1024 devices in a mesh: row: 16 (over x, y), col: 64 (over z, core).
Axes of the slice: x: 4, y: 4, z: 32, core: 2. Of those that a mesh axis runs over, the one named last changes fastest.
Arguments:
- omega_sq: float32 [8192, 8192], P('row', 'col'), may hold values from -6 to 6
- pole_freq: float32 [8192, 8192], P('row', 'col'), may hold values from 0.5 to 4
- mtx_left: float32 [1, 8192, 128], P(None, ('row', 'col')), may hold values from -0.0625 to 0.0625
- mtx_right: float32 [1, 8192, 128], P(None, ('col', 'row')), may hold values from -0.0625 to 0.0625
- band_ids: int32 [1], replicated, may hold values from 0 to 63
- band_energy: float32 [64], replicated, may hold values from -3 to 1
- eval_energy: float32 [3], replicated, may hold values from -1 to 1
Outputs:
- sigma: float32 [128, 384], replicated
The draws below stay inside these ranges and needn't reach their ends.
All inputs are finite; a program needn't handle non-finite values.
Results may differ from the reference program's by a relative error of at most 0.0001.
Values sent between devices are 32-bit elements; how exact they have to be, the bound alone decides.
No kernel may reach another device: no remote copies, remote signals or barrier semaphores. Data moves between devices by JAX's collectives and lax.ppermute only.
A program may use at most 32 MiB of HBM per device.

```python
import math
import jax
import jax.numpy as jnp
from jax import lax

NG = 8192
NS = 128
NE = 3
NBAND = 1
NSTORE = 64


def steps_of(key, shape, cuts, low, top_value):
    level = 1.0
    for position, blocks in cuts:
        heights = jax.random.uniform(jax.random.fold_in(jax.random.fold_in(key, 6), position), (blocks,), jnp.float32, low / len(cuts), top_value / len(cuts))
        level = level * jnp.repeat(jnp.exp(heights), shape[position] // blocks).reshape((-1,) + (1,) * (len(shape) - 1 - position))
    return level


def normal_values(key, extent, width, bound, shards=(), held_as=jnp.bfloat16):
    values = jax.random.normal(key, extent, jnp.float32) * width
    if len(shards) > 0:
        values = steps_of(key, extent, shards, -0.22, 0.18) * values
    return jnp.clip(values, min=-bound, max=bound).astype(held_as)


def setup_inputs(seed: int = 0) -> dict:
    arg_keys = jax.random.split(jax.random.key(seed), 8)
    return {
        "omega_sq": normal_values(arg_keys[0], (NG, NG), 1.0, 6.0, ((0, 16), (1, 64)), jnp.float32),
        "pole_freq": jnp.clip(jnp.exp(math.log(4.0) - 2.0794415 * jax.random.uniform(arg_keys[1], (NG, NG), jnp.float32) ** steps_of(arg_keys[1], (NG, NG), ((0, 16), (1, 64)), -0.2, 0.2)), 0.5, 4.0),
        "mtx_left": normal_values(arg_keys[2], (NBAND, NG, NS), NG ** -0.5, 0.0625, ((1, 1024),), jnp.float32),
        "mtx_right": normal_values(arg_keys[3], (NBAND, NG, NS), NG ** -0.5, 0.0625, ((1, 1024),), jnp.float32),
        "band_ids": jax.random.randint(arg_keys[4], (NBAND,), 0, NSTORE).astype(jnp.int32),
        "band_energy": jnp.clip(jax.random.uniform(arg_keys[5], (NSTORE,), jnp.float32, -3.0, 1.0), -3.0, 1.0),
        "eval_energy": jnp.clip(jax.random.uniform(arg_keys[6], (NE,), jnp.float32, -1.0, 1.0), -1.0, 1.0),
    }


def reference(omega_sq, pole_freq, mtx_left, mtx_right, band_ids, band_energy, eval_energy):
    hits = (band_ids[:, None] == jnp.arange(band_energy.shape[0], dtype=jnp.int32)[None, :]).astype(band_energy.dtype)
    levels = jnp.sum(hits * band_energy[None, :], axis=1)
    shifts = eval_energy[None, :] - levels[:, None]
    blocks = 16
    rows = NG // blocks
    omega_blocks = omega_sq.reshape(blocks, rows, NG)
    freq_blocks = pole_freq.reshape(blocks, rows, NG)
    left_blocks = jnp.transpose(mtx_left.reshape(NBAND, blocks, rows, NS), (1, 0, 2, 3))

    def step(total, pieces):
        omega_rows, freq_rows, left_rows = pieces
        ratio = omega_rows / freq_rows
        for band in range(NBAND):
            parts = []
            for energy in range(NE):
                gap = shifts[band, energy] - freq_rows
                kern = ratio * gap / (gap * gap + 0.09)
                parts.append(jnp.dot(kern, mtx_right[band], preferred_element_type=jnp.float32, precision=lax.Precision.HIGHEST))
            product = jnp.concatenate(parts, axis=1)
            total = total + lax.dot_general(left_rows[band], product, (((0,), (0,)), ((), ())), precision=lax.Precision.HIGHEST, preferred_element_type=jnp.float32)
        return total, None

    start = jnp.zeros((NS, NE * NS), omega_sq.dtype)
    total, unused = lax.scan(step, start, (omega_blocks, freq_blocks, left_blocks))
    return total
```

```python
import jax
import jax.numpy as jnp
from jax import lax
from jax.sharding import Mesh, PartitionSpec as P

ROW = ("x", "y")
COL = ("z_hi", "z_mid", "z_lo", "core")


def contract_rows(left, right):
    return lax.dot_general(
        left,
        right,
        (((0,), (0,)), ((), ())),
        precision=lax.Precision.HIGHEST,
        preferred_element_type=jnp.float32,
    )


def kernel_rows(ratio, freq, shift_row, right_cols, energies):
    parts = []
    for energy in range(energies):
        gap = shift_row[energy] - freq
        kern = ratio * gap / (gap * gap + 0.09)
        parts.append(
            jnp.dot(
                kern,
                right_cols,
                preferred_element_type=jnp.float32,
                precision=lax.Precision.HIGHEST,
            )
        )
    return jnp.concatenate(parts, axis=1)


def gather(block, axes):
    size = lax.axis_size(axes)
    return lax.all_to_all(jnp.broadcast_to(block, (size, *block.shape)), axes, 0, 0)


def sum_everywhere(total, near, far):
    rows, columns = total.shape
    size = lax.axis_size(near)
    pieces = lax.all_to_all(total.reshape(size, rows // size, columns), near, 0, 0)
    piece = jnp.sum(gather(jnp.sum(pieces, axis=0), far), axis=0)
    return gather(piece, near).reshape(rows, columns)


def shards(omega_sq, pole_freq, mtx_left, mtx_right, band_ids, band_energy, eval_energy):
    table = band_energy.shape[0]
    energies = eval_energy.shape[0]
    states = mtx_left.shape[2]
    hits = (band_ids[:, None] == jnp.arange(table, dtype=jnp.int32)[None, :]).astype(jnp.float32)
    levels = jnp.sum(hits * band_energy[None, :], axis=1)
    shifts = eval_energy[None, :] - levels[:, None]
    left_far = gather(mtx_left[0], ("z_hi", "z_mid"))
    left_near = gather(left_far, ("z_lo", "core"))
    left_rows = jnp.transpose(left_near, (1, 0, 2, 3)).reshape(-1, states)
    ratio = omega_sq / pole_freq
    shift_row = shifts[0]
    right_cols = gather(mtx_right[0], ROW).reshape(-1, states)
    product = kernel_rows(ratio, pole_freq, shift_row, right_cols, energies)
    total = contract_rows(left_rows, product)
    return sum_everywhere(total, (*ROW, "z_lo", "core"), ("z_hi", "z_mid"))


def solution(mesh):
    split = Mesh(mesh.devices.reshape(4, 4, 8, 2, 2, 2), (*ROW, *COL))
    return jax.shard_map(
        shards,
        mesh=split,
        in_specs=(
            P(ROW, COL),
            P(ROW, COL),
            P(None, (*ROW, *COL), None),
            P(None, (*COL, *ROW), None),
            P(),
            P(),
            P(),
        ),
        out_specs=P(),
        check_vma=False,
    )
```

```python
import jax
import jax.numpy as jnp
from jax import lax
from jax.sharding import Mesh, PartitionSpec as P


ROW = ("x", "y")
COL = ("z_hi", "z_mid", "z_lo", "core")


def contract_rows(left, right):
    return lax.dot_general(
        left,
        right,
        (((0,), (0,)), ((), ())),
        precision=lax.Precision.HIGHEST,
        preferred_element_type=jnp.float32,
    )


def kernel_rows(ratio, freq, shift_row, right_cols, energies):
    parts = []
    for energy in range(energies):
        gap = shift_row[energy] - freq
        kern = ratio * gap / (gap * gap + 0.09)
        parts.append(
            jnp.dot(
                kern,
                right_cols,
                preferred_element_type=jnp.float32,
                precision=lax.Precision.HIGHEST,
            )
        )
    return jnp.concatenate(parts, axis=1)


def gather(block, axes):
    size = lax.axis_size(axes)
    return lax.all_to_all(jnp.broadcast_to(block, (size, *block.shape)), axes, 0, 0)


def sum_everywhere(total, near, far):
    rows, columns = total.shape
    size = lax.axis_size(near)
    pieces = lax.all_to_all(total.reshape(size, rows // size, columns), near, 0, 0)
    piece = jnp.sum(gather(jnp.sum(pieces, axis=0), far), axis=0)
    return gather(piece, near).reshape(rows, columns)


def shards(omega_sq, pole_freq, mtx_left, mtx_right, band_ids, band_energy, eval_energy):
    table = band_energy.shape[0]
    energies = eval_energy.shape[0]
    states = mtx_left.shape[2]
    hits = (band_ids[:, None] == jnp.arange(table, dtype=jnp.int32)[None, :]).astype(jnp.float32)
    levels = jnp.sum(hits * band_energy[None, :], axis=1)
    shifts = eval_energy[None, :] - levels[:, None]
    left_rows = gather(mtx_left[0], COL[:-1]).reshape(-1, states)
    ratio = omega_sq / pole_freq
    shift_row = shifts[0]
    right_cols = gather(mtx_right[0], ROW).reshape(-1, states)
    product = kernel_rows(ratio, pole_freq, shift_row, right_cols, energies)
    core = lax.axis_index("core")
    halves = product.reshape(-1, 2, mtx_left.shape[1], energies * states)
    other = lax.ppermute(lax.dynamic_index_in_dim(halves, 1 - core, 1, keepdims=False), "core", ((0, 1), (1, 0)))
    half = lax.dynamic_index_in_dim(halves, core, 1, keepdims=False) + other
    total = contract_rows(left_rows, half.reshape(-1, energies * states))
    return sum_everywhere(total, (*ROW, "z_lo", "core"), ("z_hi", "z_mid"))


def solution(mesh):
    split = Mesh(mesh.devices.reshape(4, 4, 8, 2, 2, 2), (*ROW, *COL))
    return jax.shard_map(
        shards,
        mesh=split,
        in_specs=(
            P(ROW, COL),
            P(ROW, COL),
            P(None, (*ROW, *COL), None),
            P(None, (*COL, *ROW), None),
            P(),
            P(),
            P(),
        ),
        out_specs=P(),
        check_vma=False,
    )
```

```python
import functools

import jax
import jax.numpy as jnp
from jax import lax
from jax.experimental import pallas as pl
from jax.experimental.pallas import tpu as pltpu
from jax.sharding import Mesh, PartitionSpec as P


ROW = ("x", "y")
COL = ("z_far", "z_lo", "core")
NEAR = (*ROW, "z_lo", "core")


def contract_rows(left, right):
    return lax.dot_general(
        left,
        right,
        (((0,), (0,)), ((), ())),
        precision=lax.Precision.HIGHEST,
        preferred_element_type=jnp.float32,
    )


def product_body(which_ref, shift_ref, omega_ref, freq_ref, right_ref, out_ref):
    which = which_ref[0]
    depth = freq_ref.shape[-1]
    states = right_ref.shape[1]
    freq = freq_ref[:, which].reshape(-1, depth)
    ratio = omega_ref[:, which].reshape(-1, depth) / freq
    for energy in range(shift_ref.shape[0]):
        gap = shift_ref[energy, 0:1, :] - freq
        kern = ratio * gap / (gap * gap + 0.09)
        out_ref[:, energy * states : (energy + 1) * states] = jnp.dot(
            kern,
            right_ref[...],
            preferred_element_type=jnp.float32,
            precision=lax.Precision.HIGHEST,
        )


def product_half(which, shifts, omega, freq, right_cols):
    chips, _, rows, depth = omega.shape
    energies = shifts.shape[0]
    states = right_cols.shape[1]
    vmem = pl.BlockSpec(memory_space=pltpu.VMEM)
    return pl.pallas_call(
        product_body,
        name="product_half",
        out_shape=jax.ShapeDtypeStruct((chips * rows, energies * states), jnp.float32),
        in_specs=[pl.BlockSpec(memory_space=pltpu.SMEM), vmem, vmem, vmem, vmem],
        out_specs=vmem,
        compiler_params=pltpu.CompilerParams(vmem_limit_bytes=8 << 20),
        cost_estimate=pl.CostEstimate(
            flops=2 * chips * rows * depth * states * energies,
            bytes_accessed=4 * (2 * omega.size + chips * rows * energies * states),
            transcendentals=0,
        ),
    )(jnp.reshape(which, (1,)), shifts, omega, freq, right_cols)


def gather(block, axes):
    size = lax.axis_size(axes)
    return lax.all_to_all(jnp.broadcast_to(block, (size, *block.shape)), axes, 0, 0)


def add_swapped(mine, theirs, axis):
    return mine + lax.ppermute(theirs, axis, ((0, 1), (1, 0)))


def sum_everywhere(total, near, far):
    rows, columns = total.shape
    size = lax.axis_size(near)
    pieces = lax.all_to_all(total.reshape(size, rows // size, columns), near, 0, 0)
    piece = jnp.sum(gather(jnp.sum(pieces, axis=0), far), axis=0)
    return gather(piece, near).reshape(rows, columns)


def shards(omega_sq, pole_freq, mtx_left, mtx_right, band_ids, band_energy, eval_energy):
    table = band_energy.shape[0]
    energies = eval_energy.shape[0]
    rows, states = mtx_left.shape[1:]
    depth = pole_freq.shape[1]
    hits = (band_ids[:, None] == jnp.arange(table, dtype=jnp.int32)[None, :]).astype(jnp.float32)
    levels = jnp.sum(hits * band_energy[None, :], axis=1)
    shifts = eval_energy[None, :] - levels[:, None]
    shift_rows = jnp.broadcast_to(shifts[0][:, None, None], (energies, 8, depth))
    core = lax.axis_index("core")
    z_lo = lax.axis_index("z_lo")
    blocks = (-1, 2, rows, depth)
    omega, freq = omega_sq.reshape(blocks), pole_freq.reshape(blocks)
    left_rows = gather(mtx_left[0], "z_far").reshape(-1, states)
    right_cols = gather(mtx_right[0], ROW).reshape(-1, states)
    half = functools.partial(
        product_half, shifts=shift_rows, omega=omega, freq=freq, right_cols=right_cols
    )
    theirs = half(1 - core)
    mine = half(core)
    mine = add_swapped(mine, theirs, "core")
    quarters = mine.reshape(-1, 2, rows, energies * states)
    quarter = functools.partial(lax.dynamic_index_in_dim, quarters, axis=1, keepdims=False)
    product = add_swapped(quarter(z_lo), quarter(1 - z_lo), "z_lo")
    total = contract_rows(left_rows, product.reshape(-1, energies * states))
    return sum_everywhere(total, NEAR, "z_far")


def solution(mesh):
    split = Mesh(mesh.devices.reshape(4, 4, 16, 2, 2), (*ROW, *COL))
    return jax.shard_map(
        shards,
        mesh=split,
        in_specs=(
            P(ROW, COL),
            P(ROW, COL),
            P(None, (*ROW, *COL), None),
            P(None, (*COL, *ROW), None),
            P(),
            P(),
            P(),
        ),
        out_specs=P(),
        check_vma=False,
    )
```

```python
import jax
import jax.numpy as jnp
from jax import lax
from jax.sharding import Mesh, PartitionSpec as P


ROW = ("x", "y")
COL = ("z_far", "z_lo", "core")
NEAR = (*ROW, "z_lo", "core")
ROW_FIRST = 2 * 4 + 2
NEAR_FIRST = (ROW_FIRST * 2 + 1) * 2
FAR_FIRST = 8
Z_FIRST = 16


def contract_rows(left, right):
    return lax.dot_general(
        left,
        right,
        (((0,), (0,)), ((), ())),
        precision=lax.Precision.HIGHEST,
        preferred_element_type=jnp.float32,
    )


def kernel_rows(ratio, freq, shift_row, right_cols, energies):
    parts = []
    for energy in range(energies):
        gap = shift_row[energy] - freq
        kern = ratio * gap / (gap * gap + 0.09)
        parts.append(
            jnp.dot(
                kern,
                right_cols,
                preferred_element_type=jnp.float32,
                precision=lax.Precision.HIGHEST,
            )
        )
    return jnp.concatenate(parts, axis=1)


def exchange(pieces, axes, first):
    size = pieces.shape[0]
    order = [(first + i) % size for i in range(size)]
    return lax.all_to_all(pieces, axes, 0, 0, axis_index_groups=[order])


def gather(block, axes, first):
    size = lax.axis_size(axes)
    return exchange(jnp.broadcast_to(block, (size, *block.shape)), axes, first)


def sum_everywhere(total):
    rows, columns = total.shape
    size = lax.axis_size(NEAR)
    pieces = exchange(total.reshape(size, rows // size, columns), NEAR, NEAR_FIRST)
    piece = jnp.sum(gather(jnp.sum(pieces, axis=0), "z_far", FAR_FIRST), axis=0)
    return gather(piece, NEAR, NEAR_FIRST).reshape(rows, columns)


def shards(omega_sq, pole_freq, mtx_left, mtx_right, band_ids, band_energy, eval_energy):
    table = band_energy.shape[0]
    energies = eval_energy.shape[0]
    states = mtx_left.shape[2]
    hits = (band_ids[:, None] == jnp.arange(table, dtype=jnp.int32)[None, :]).astype(jnp.float32)
    levels = jnp.sum(hits * band_energy[None, :], axis=1)
    shifts = eval_energy[None, :] - levels[:, None]
    left_blocks = gather(mtx_left[0], COL[:-1], Z_FIRST)
    ratio = omega_sq / pole_freq
    shift_row = shifts[0]
    right_blocks = gather(mtx_right[0], ROW, ROW_FIRST)
    right_cols = jnp.roll(right_blocks, ROW_FIRST, axis=0).reshape(-1, states)
    product = kernel_rows(ratio, pole_freq, shift_row, right_cols, energies)
    core = lax.axis_index("core")
    halves = product.reshape(-1, 2, mtx_left.shape[1], energies * states)
    other = lax.ppermute(
        lax.dynamic_index_in_dim(halves, 1 - core, 1, keepdims=False), "core", ((0, 1), (1, 0))
    )
    half = lax.dynamic_index_in_dim(halves, core, 1, keepdims=False) + other
    left_rows = jnp.roll(left_blocks, Z_FIRST, axis=0).reshape(-1, states)
    total = contract_rows(left_rows, half.reshape(-1, energies * states))
    return sum_everywhere(total)


def solution(mesh):
    split = Mesh(mesh.devices.reshape(4, 4, 16, 2, 2), (*ROW, *COL))
    return jax.shard_map(
        shards,
        mesh=split,
        in_specs=(
            P(ROW, COL),
            P(ROW, COL),
            P(None, (*ROW, *COL), None),
            P(None, (*COL, *ROW), None),
            P(),
            P(),
            P(),
        ),
        out_specs=P(),
        check_vma=False,
    )
```

```python
import jax
import jax.numpy as jnp
from jax import lax
from jax.experimental import pallas as pl
from jax.experimental.pallas import tpu as pltpu
from jax.sharding import Mesh, PartitionSpec as P


ROW = ("x", "y")
COL = ("z_far", "z_lo", "core")
NEAR = (*ROW, "z_lo", "core")
ROW_FIRST = 2 * 4 + 2
NEAR_FIRST = (ROW_FIRST * 2 + 1) * 2
FAR_FIRST = 8


def dot(left, right):
    return jnp.dot(
        left,
        right,
        precision=lax.Precision.HIGHEST,
        preferred_element_type=jnp.float32,
    )


def block_body(place_ref, shift_ref, omega_ref, freq_ref, mine_ref, other_ref, right_ref, out_ref, left_ref):
    z_lo, core = place_ref[0], place_ref[1]
    chips = left_ref.shape[0]
    states = right_ref.shape[1]
    for blocks, at_core in ((mine_ref, core), (other_ref, 1 - core)):
        for i, at_z in enumerate((z_lo, 1 - z_lo)):
            left_ref[:FAR_FIRST, at_z, at_core] = blocks[i, chips - FAR_FIRST :]
            left_ref[FAR_FIRST:, at_z, at_core] = blocks[i, : chips - FAR_FIRST]
    left = left_ref[...].reshape(-1, states).T
    freq = freq_ref[...]
    ratio = omega_ref[...] / freq
    for energy in range(shift_ref.shape[0]):
        gap = shift_ref[energy, 0:1, :] - freq
        kern = ratio * gap / (gap * gap + 0.09)
        out_ref[:, energy * states : (energy + 1) * states] = dot(dot(left, kern), right_ref[...])


def block_sum(place, shifts, omega, freq, mine, other, right_cols):
    rows, depth = freq.shape
    energies = shifts.shape[0]
    states = right_cols.shape[1]
    pair, chips, lines, _ = mine.shape
    vmem = pl.BlockSpec(memory_space=pltpu.VMEM)
    return pl.pallas_call(
        block_body,
        name="block_sum",
        out_shape=jax.ShapeDtypeStruct((states, energies * states), jnp.float32),
        in_specs=[pl.BlockSpec(memory_space=pltpu.SMEM)] + [vmem] * 6,
        out_specs=vmem,
        scratch_shapes=[pltpu.VMEM((chips, pair, 2, lines, states), jnp.float32)],
        compiler_params=pltpu.CompilerParams(vmem_limit_bytes=16 << 20),
        cost_estimate=pl.CostEstimate(
            flops=2 * (rows + depth) * depth * states * energies,
            bytes_accessed=4 * (3 * freq.size + energies * states * states),
            transcendentals=0,
        ),
    )(place, shifts, omega, freq, mine, other, right_cols)


def exchange(pieces, axes, first):
    size = pieces.shape[0]
    order = [(first + i) % size for i in range(size)]
    return lax.all_to_all(pieces, axes, 0, 0, axis_index_groups=[order])


def gather(block, axes, first):
    size = lax.axis_size(axes)
    return exchange(jnp.broadcast_to(block, (size, *block.shape)), axes, first)


def sum_everywhere(total):
    rows, columns = total.shape
    size = lax.axis_size(NEAR)
    pieces = exchange(total.reshape(size, rows // size, columns), NEAR, NEAR_FIRST)
    piece = jnp.sum(gather(jnp.sum(pieces, axis=0), "z_far", FAR_FIRST), axis=0)
    return gather(piece, NEAR, NEAR_FIRST).reshape(rows, columns)


def with_partner(blocks, axis):
    return jnp.stack([blocks, lax.ppermute(blocks, axis, ((0, 1), (1, 0)))])


def shards(omega_sq, pole_freq, mtx_left, mtx_right, band_ids, band_energy, eval_energy):
    table = band_energy.shape[0]
    energies = eval_energy.shape[0]
    states = mtx_left.shape[2]
    depth = pole_freq.shape[1]
    hits = (band_ids[:, None] == jnp.arange(table, dtype=jnp.int32)[None, :]).astype(jnp.float32)
    levels = jnp.sum(hits * band_energy[None, :], axis=1)
    shifts = eval_energy[None, :] - levels[:, None]
    shift_rows = jnp.broadcast_to(shifts[0][:, None, None], (energies, 8, depth))
    place = jnp.stack([lax.axis_index("z_lo"), lax.axis_index("core")])
    left_far = gather(mtx_left[0], "z_far", FAR_FIRST)
    mine = with_partner(left_far, "z_lo")
    other = lax.ppermute(mine, "core", ((0, 1), (1, 0)))
    right_blocks = gather(mtx_right[0], ROW, ROW_FIRST)
    right_cols = jnp.roll(right_blocks, ROW_FIRST, axis=0).reshape(-1, states)
    total = block_sum(place, shift_rows, omega_sq, pole_freq, mine, other, right_cols)
    return sum_everywhere(total)


def solution(mesh):
    split = Mesh(mesh.devices.reshape(4, 4, 16, 2, 2), (*ROW, *COL))
    return jax.shard_map(
        shards,
        mesh=split,
        in_specs=(
            P(ROW, COL),
            P(ROW, COL),
            P(None, (*ROW, *COL), None),
            P(None, (*COL, *ROW), None),
            P(),
            P(),
            P(),
        ),
        out_specs=P(),
        check_vma=False,
    )
```

```python
import jax
import jax.numpy as jnp
from jax import lax
from jax.experimental import pallas as pl
from jax.experimental.pallas import tpu as pltpu
from jax.sharding import Mesh, PartitionSpec as P


ROW = ("x", "y")
COL = ("z_far", "z_lo", "core")
NEAR = (*ROW, "z_lo", "core")
ROW_FIRST = 2 * 4 + 2
NEAR_FIRST = (ROW_FIRST * 2 + 1) * 2
FAR_FIRST = 8


def dot(left, right):
    return jnp.dot(
        left,
        right,
        precision=lax.Precision.HIGHEST,
        preferred_element_type=jnp.float32,
    )


def half_terms(z_lo, core, shift_ref, omega_ref, freq_ref, blocks_ref, left_ref):
    chips = left_ref.shape[0]
    depth = freq_ref.shape[-1]
    for i, at_z in enumerate((z_lo, 1 - z_lo)):
        left_ref[:FAR_FIRST, at_z] = blocks_ref[i, chips - FAR_FIRST :]
        left_ref[FAR_FIRST:, at_z] = blocks_ref[i, : chips - FAR_FIRST]
    left = left_ref[...].reshape(-1, left_ref.shape[-1]).T
    freq = freq_ref[:, core].reshape(-1, depth)
    ratio = omega_ref[:, core].reshape(-1, depth) / freq
    for energy in range(shift_ref.shape[0]):
        gap = shift_ref[energy, 0:1, :] - freq
        yield dot(left, ratio * gap / (gap * gap + 0.09))


def mine_body(place_ref, shift_ref, omega_ref, freq_ref, mine_ref, out_ref, left_ref):
    z_lo, core = place_ref[0], place_ref[1]
    terms = half_terms(z_lo, core, shift_ref, omega_ref, freq_ref, mine_ref, left_ref)
    for energy, term in enumerate(terms):
        out_ref[energy] = term


def rest_body(place_ref, shift_ref, omega_ref, freq_ref, other_ref, part_ref, right_ref, out_ref, left_ref):
    z_lo, core = place_ref[0], place_ref[1]
    states = right_ref.shape[1]
    terms = half_terms(z_lo, 1 - core, shift_ref, omega_ref, freq_ref, other_ref, left_ref)
    for energy, term in enumerate(terms):
        out_ref[:, energy * states : (energy + 1) * states] = dot(part_ref[energy] + term, right_ref[...])


def local_kernel(body, out_shape, place, shifts, omega, freq, blocks, *more):
    lines, depth = blocks.shape[2:]
    energies = shifts.shape[0]
    vmem = pl.BlockSpec(memory_space=pltpu.VMEM)
    return pl.pallas_call(
        body,
        out_shape=jax.ShapeDtypeStruct(out_shape, jnp.float32),
        in_specs=[pl.BlockSpec(memory_space=pltpu.SMEM)] + [vmem] * (4 + len(more)),
        out_specs=vmem,
        scratch_shapes=[pltpu.VMEM((blocks.shape[1], blocks.shape[0], lines, depth), jnp.float32)],
        compiler_params=pltpu.CompilerParams(vmem_limit_bytes=16 << 20),
        cost_estimate=pl.CostEstimate(
            flops=omega.size * depth * energies,
            bytes_accessed=4 * (2 * omega.size + blocks.size + energies * depth * depth),
            transcendentals=0,
        ),
    )(place, shifts, omega, freq, blocks, *more)


def exchange(pieces, axes, first):
    size = pieces.shape[0]
    order = [(first + i) % size for i in range(size)]
    return lax.all_to_all(pieces, axes, 0, 0, axis_index_groups=[order])


def gather(block, axes, first):
    size = lax.axis_size(axes)
    return exchange(jnp.broadcast_to(block, (size, *block.shape)), axes, first)


def sum_everywhere(total):
    rows, columns = total.shape
    size = lax.axis_size(NEAR)
    pieces = exchange(total.reshape(size, rows // size, columns), NEAR, NEAR_FIRST)
    piece = jnp.sum(gather(jnp.sum(pieces, axis=0), "z_far", FAR_FIRST), axis=0)
    return gather(piece, NEAR, NEAR_FIRST).reshape(rows, columns)


def with_partner(blocks, axis):
    return jnp.stack([blocks, lax.ppermute(blocks, axis, ((0, 1), (1, 0)))])


def shards(omega_sq, pole_freq, mtx_left, mtx_right, band_ids, band_energy, eval_energy):
    table = band_energy.shape[0]
    energies = eval_energy.shape[0]
    states = mtx_left.shape[2]
    depth = pole_freq.shape[1]
    place = jnp.stack([lax.axis_index("z_lo"), lax.axis_index("core")])
    pairs = (-1, 2, mtx_left.shape[1], depth)
    omega, freq = omega_sq.reshape(pairs), pole_freq.reshape(pairs)
    hits = (band_ids[:, None] == jnp.arange(table, dtype=jnp.int32)[None, :]).astype(jnp.float32)
    levels = jnp.sum(hits * band_energy[None, :], axis=1)
    shifts = eval_energy[None, :] - levels[:, None]
    shift_rows = jnp.broadcast_to(shifts[0][:, None, None], (energies, 8, depth))
    left_far = gather(mtx_left[0], "z_far", FAR_FIRST)
    mine = with_partner(left_far, "z_lo")
    other = lax.ppermute(mine, "core", ((0, 1), (1, 0)))
    right_blocks = gather(mtx_right[0], ROW, ROW_FIRST)
    right_cols = jnp.roll(right_blocks, ROW_FIRST, axis=0).reshape(-1, states)
    arrays = (place, shift_rows, omega, freq)
    part = local_kernel(mine_body, (energies, states, depth), *arrays, mine)
    shape = (states, energies * states)
    total = local_kernel(rest_body, shape, *arrays, other, part, right_cols)
    return sum_everywhere(total)


def solution(mesh):
    split = Mesh(mesh.devices.reshape(4, 4, 16, 2, 2), (*ROW, *COL))
    return jax.shard_map(
        shards,
        mesh=split,
        in_specs=(
            P(ROW, COL),
            P(ROW, COL),
            P(None, (*ROW, *COL), None),
            P(None, (*COL, *ROW), None),
            P(),
            P(),
            P(),
        ),
        out_specs=P(),
        check_vma=False,
    )
```

```python
import jax
import jax.numpy as jnp
from jax import lax
from jax.experimental import pallas as pl
from jax.experimental.pallas import tpu as pltpu
from jax.sharding import Mesh, PartitionSpec as P


ROW = ("x", "y")
COL = ("z_far", "z_lo", "core")
NEAR = (*ROW, "z_lo", "core")
ROW_FIRST = 2 * 4 + 2
NEAR_FIRST = (ROW_FIRST * 2 + 1) * 2
FAR_FIRST = 8


def dot(left, right):
    return jnp.dot(
        left,
        right,
        precision=lax.Precision.HIGHEST,
        preferred_element_type=jnp.float32,
    )


def half_terms(z_lo, core, shift_ref, omega_ref, freq_ref, blocks_ref, left_ref):
    chips = left_ref.shape[0]
    depth = freq_ref.shape[-1]
    for i, at_z in enumerate((z_lo, 1 - z_lo)):
        left_ref[:FAR_FIRST, at_z] = blocks_ref[i, chips - FAR_FIRST :]
        left_ref[FAR_FIRST:, at_z] = blocks_ref[i, : chips - FAR_FIRST]
    left = left_ref[...].reshape(-1, left_ref.shape[-1]).T
    freq = freq_ref[:, core].reshape(-1, depth)
    ratio = omega_ref[:, core].reshape(-1, depth) / freq
    for energy in range(shift_ref.shape[0]):
        gap = shift_ref[energy, 0:1, :] - freq
        yield dot(left, ratio * gap / (gap * gap + 0.09))


def mine_body(place_ref, shift_ref, omega_ref, freq_ref, mine_ref, out_ref, left_ref):
    z_lo, core = place_ref[0], place_ref[1]
    terms = half_terms(z_lo, core, shift_ref, omega_ref, freq_ref, mine_ref, left_ref)
    for energy, term in enumerate(terms):
        out_ref[energy] = term


def rest_body(place_ref, shift_ref, omega_ref, freq_ref, other_ref, part_ref, out_ref, left_ref):
    z_lo, core = place_ref[0], place_ref[1]
    terms = half_terms(z_lo, 1 - core, shift_ref, omega_ref, freq_ref, other_ref, left_ref)
    for energy, term in enumerate(terms):
        out_ref[energy] = part_ref[energy] + term


def last_body(part_ref, right_ref, out_ref):
    states = right_ref.shape[1]
    for energy in range(part_ref.shape[0]):
        out_ref[:, energy * states : (energy + 1) * states] = dot(part_ref[energy], right_ref[...])


def last_kernel(part, right_cols):
    energies, states, _ = part.shape
    vmem = pl.BlockSpec(memory_space=pltpu.VMEM)
    return pl.pallas_call(
        last_body,
        name="last",
        out_shape=jax.ShapeDtypeStruct((states, energies * right_cols.shape[1]), jnp.float32),
        in_specs=[vmem, vmem],
        out_specs=vmem,
        compiler_params=pltpu.CompilerParams(vmem_limit_bytes=16 << 20),
        cost_estimate=pl.CostEstimate(
            flops=2 * part.size * right_cols.shape[1],
            bytes_accessed=4 * (2 * part.size + right_cols.size),
            transcendentals=0,
        ),
    )(part, right_cols)


def local_kernel(body, out_shape, place, shifts, omega, freq, blocks, *more):
    lines, depth = blocks.shape[2:]
    energies = shifts.shape[0]
    vmem = pl.BlockSpec(memory_space=pltpu.VMEM)
    return pl.pallas_call(
        body,
        out_shape=jax.ShapeDtypeStruct(out_shape, jnp.float32),
        in_specs=[pl.BlockSpec(memory_space=pltpu.SMEM)] + [vmem] * (4 + len(more)),
        out_specs=vmem,
        scratch_shapes=[pltpu.VMEM((blocks.shape[1], blocks.shape[0], lines, depth), jnp.float32)],
        compiler_params=pltpu.CompilerParams(vmem_limit_bytes=16 << 20),
        cost_estimate=pl.CostEstimate(
            flops=omega.size * depth * energies,
            bytes_accessed=4 * (2 * omega.size + blocks.size + energies * depth * depth),
            transcendentals=0,
        ),
    )(place, shifts, omega, freq, blocks, *more)


def exchange(pieces, axes, first):
    size = pieces.shape[0]
    order = [(first + i) % size for i in range(size)]
    return lax.all_to_all(pieces, axes, 0, 0, axis_index_groups=[order])


def gather(block, axes, first):
    size = lax.axis_size(axes)
    return exchange(jnp.broadcast_to(block, (size, *block.shape)), axes, first)


def sum_everywhere(total):
    rows, columns = total.shape
    size = lax.axis_size(NEAR)
    pieces = exchange(total.reshape(size, rows // size, columns), NEAR, NEAR_FIRST)
    piece = jnp.sum(gather(jnp.sum(pieces, axis=0), "z_far", FAR_FIRST), axis=0)
    return gather(piece, NEAR, NEAR_FIRST).reshape(rows, columns)


def with_partner(blocks, axis):
    return jnp.stack([blocks, lax.ppermute(blocks, axis, ((0, 1), (1, 0)))])


def shards(omega_sq, pole_freq, mtx_left, mtx_right, band_ids, band_energy, eval_energy):
    table = band_energy.shape[0]
    energies = eval_energy.shape[0]
    states = mtx_left.shape[2]
    depth = pole_freq.shape[1]
    place = jnp.stack([lax.axis_index("z_lo"), lax.axis_index("core")])
    pairs = (-1, 2, mtx_left.shape[1], depth)
    omega, freq = omega_sq.reshape(pairs), pole_freq.reshape(pairs)
    hits = (band_ids[:, None] == jnp.arange(table, dtype=jnp.int32)[None, :]).astype(jnp.float32)
    levels = jnp.sum(hits * band_energy[None, :], axis=1)
    shifts = eval_energy[None, :] - levels[:, None]
    shift_rows = jnp.broadcast_to(shifts[0][:, None, None], (energies, 8, depth))
    left_far = gather(mtx_left[0], "z_far", FAR_FIRST)
    mine = with_partner(left_far, "z_lo")
    other = lax.ppermute(mine, "core", ((0, 1), (1, 0)))
    right_blocks = gather(mtx_right[0], ROW, ROW_FIRST)
    right_cols = jnp.roll(right_blocks, ROW_FIRST, axis=0).reshape(-1, states)
    arrays = (place, shift_rows, omega, freq)
    part = local_kernel(mine_body, (energies, states, depth), *arrays, mine)
    part = local_kernel(rest_body, part.shape, *arrays, other, part)
    total = last_kernel(part, right_cols)
    return sum_everywhere(total)


def solution(mesh):
    split = Mesh(mesh.devices.reshape(4, 4, 16, 2, 2), (*ROW, *COL))
    return jax.shard_map(
        shards,
        mesh=split,
        in_specs=(
            P(ROW, COL),
            P(ROW, COL),
            P(None, (*ROW, *COL), None),
            P(None, (*COL, *ROW), None),
            P(),
            P(),
            P(),
        ),
        out_specs=P(),
        check_vma=False,
    )
```

```python
import jax
import jax.numpy as jnp
from jax import lax
from jax.experimental import pallas as pl
from jax.experimental.pallas import tpu as pltpu
from jax.sharding import Mesh, PartitionSpec as P


ROW = ("x", "y")
COL = ("z_far", "z_lo", "core")
NEAR = (*ROW, "z_lo", "core")
ROW_FIRST = 2 * 4 + 2
NEAR_FIRST = (ROW_FIRST * 2 + 1) * 2
FAR_FIRST = 8


def dot(left, right):
    return jnp.dot(
        left,
        right,
        precision=lax.Precision.HIGHEST,
        preferred_element_type=jnp.float32,
    )


def half_terms(z_lo, core, shift_ref, omega_ref, freq_ref, blocks_ref, left_ref):
    chips = left_ref.shape[0]
    depth = freq_ref.shape[-1]
    for i, at_z in enumerate((z_lo, 1 - z_lo)):
        left_ref[:FAR_FIRST, at_z] = blocks_ref[i, chips - FAR_FIRST :]
        left_ref[FAR_FIRST:, at_z] = blocks_ref[i, : chips - FAR_FIRST]
    left = left_ref[...].reshape(-1, left_ref.shape[-1]).T
    freq = freq_ref[:, core].reshape(-1, depth)
    ratio = omega_ref[:, core].reshape(-1, depth) / freq
    for energy in range(shift_ref.shape[0]):
        gap = shift_ref[energy, 0:1, :] - freq
        yield dot(left, ratio * gap / (gap * gap + 0.09))


def mine_body(place_ref, shift_ref, omega_ref, freq_ref, mine_ref, out_ref, left_ref):
    z_lo, core = place_ref[0], place_ref[1]
    terms = half_terms(z_lo, core, shift_ref, omega_ref, freq_ref, mine_ref, left_ref)
    for energy, term in enumerate(terms):
        out_ref[energy] = term


def rest_body(place_ref, shift_ref, omega_ref, freq_ref, other_ref, part_ref, out_ref, left_ref):
    z_lo, core = place_ref[0], place_ref[1]
    terms = half_terms(z_lo, 1 - core, shift_ref, omega_ref, freq_ref, other_ref, left_ref)
    for energy, term in enumerate(terms):
        out_ref[energy] = part_ref[energy] + term


def last_body(part_ref, right_ref, out_ref):
    lines, lanes = out_ref.shape[2:]
    for energy in range(part_ref.shape[0]):
        out_ref[:, energy] = dot(part_ref[energy], right_ref[...]).reshape(-1, lines, lanes)


def last_kernel(part, right_cols):
    energies, states, _ = part.shape
    vmem = pl.BlockSpec(memory_space=pltpu.VMEM)
    return pl.pallas_call(
        last_body,
        name="last",
        out_shape=jax.ShapeDtypeStruct((states // 8, energies, 8, right_cols.shape[1]), jnp.float32),
        in_specs=[vmem, vmem],
        out_specs=vmem,
        compiler_params=pltpu.CompilerParams(vmem_limit_bytes=16 << 20),
        cost_estimate=pl.CostEstimate(
            flops=2 * part.size * right_cols.shape[1],
            bytes_accessed=4 * (2 * part.size + right_cols.size),
            transcendentals=0,
        ),
    )(part, right_cols)


def local_kernel(body, out_shape, place, shifts, omega, freq, blocks, *more):
    lines, depth = blocks.shape[2:]
    energies = shifts.shape[0]
    vmem = pl.BlockSpec(memory_space=pltpu.VMEM)
    return pl.pallas_call(
        body,
        out_shape=jax.ShapeDtypeStruct(out_shape, jnp.float32),
        in_specs=[pl.BlockSpec(memory_space=pltpu.SMEM)] + [vmem] * (4 + len(more)),
        out_specs=vmem,
        scratch_shapes=[pltpu.VMEM((blocks.shape[1], blocks.shape[0], lines, depth), jnp.float32)],
        compiler_params=pltpu.CompilerParams(vmem_limit_bytes=16 << 20),
        cost_estimate=pl.CostEstimate(
            flops=omega.size * depth * energies,
            bytes_accessed=4 * (2 * omega.size + blocks.size + energies * depth * depth),
            transcendentals=0,
        ),
    )(place, shifts, omega, freq, blocks, *more)


def exchange(pieces, axes, first):
    size = pieces.shape[0]
    order = [(first + i) % size for i in range(size)]
    return lax.all_to_all(pieces, axes, 0, 0, axis_index_groups=[order])


def gather(block, axes, first):
    size = lax.axis_size(axes)
    return exchange(jnp.broadcast_to(block, (size, *block.shape)), axes, first)


def sum_everywhere(tiles):
    size = lax.axis_size(NEAR)
    lanes = tiles.shape[-1]
    pieces = exchange(tiles.reshape(size, -1, 2, lanes), NEAR, NEAR_FIRST)
    piece = jnp.sum(gather(jnp.sum(pieces, axis=0), "z_far", FAR_FIRST), axis=0)
    return gather(piece, NEAR, NEAR_FIRST).reshape(tiles.shape)


def with_partner(blocks, axis):
    return jnp.stack([blocks, lax.ppermute(blocks, axis, ((0, 1), (1, 0)))])


def shards(omega_sq, pole_freq, mtx_left, mtx_right, band_ids, band_energy, eval_energy):
    table = band_energy.shape[0]
    energies = eval_energy.shape[0]
    states = mtx_left.shape[2]
    depth = pole_freq.shape[1]
    place = jnp.stack([lax.axis_index("z_lo"), lax.axis_index("core")])
    pairs = (-1, 2, mtx_left.shape[1], depth)
    omega, freq = omega_sq.reshape(pairs), pole_freq.reshape(pairs)
    hits = (band_ids[:, None] == jnp.arange(table, dtype=jnp.int32)[None, :]).astype(jnp.float32)
    levels = jnp.sum(hits * band_energy[None, :], axis=1)
    shifts = eval_energy[None, :] - levels[:, None]
    shift_rows = jnp.broadcast_to(shifts[0][:, None, None], (energies, 8, depth))
    left_far = gather(mtx_left[0], "z_far", FAR_FIRST)
    mine = with_partner(left_far, "z_lo")
    other = lax.ppermute(mine, "core", ((0, 1), (1, 0)))
    right_blocks = gather(mtx_right[0], ROW, ROW_FIRST)
    right_cols = jnp.roll(right_blocks, ROW_FIRST, axis=0).reshape(-1, states)
    arrays = (place, shift_rows, omega, freq)
    part = local_kernel(mine_body, (energies, states, depth), *arrays, mine)
    part = local_kernel(rest_body, part.shape, *arrays, other, part)
    tiles = last_kernel(part, right_cols)
    return sum_everywhere(tiles).transpose(0, 2, 1, 3).reshape(states, energies * states)


def solution(mesh):
    split = Mesh(mesh.devices.reshape(4, 4, 16, 2, 2), (*ROW, *COL))
    return jax.shard_map(
        shards,
        mesh=split,
        in_specs=(
            P(ROW, COL),
            P(ROW, COL),
            P(None, (*ROW, *COL), None),
            P(None, (*COL, *ROW), None),
            P(),
            P(),
            P(),
        ),
        out_specs=P(),
        check_vma=False,
    )
```

```python
import math

import jax
import jax.numpy as jnp
from jax import lax
from jax.experimental import pallas as pl
from jax.experimental.pallas import tpu as pltpu
from jax.sharding import Mesh, PartitionSpec as P


ROW = ("x", "y")
COL = ("z_far", "z_lo", "core")
NEAR = (*ROW, "z_lo", "core")
ROW_FIRST = 2 * 4 + 2
NEAR_FIRST = (ROW_FIRST * 2 + 1) * 2
FAR_FIRST = 8


def dot(left, right):
    return jnp.dot(
        left,
        right,
        precision=lax.Precision.HIGHEST,
        preferred_element_type=jnp.float32,
    )


def kern_body(shift_ref, omega_ref, freq_ref, out_ref):
    rows, depth = out_ref.shape[2:]
    for core in range(out_ref.shape[0]):
        freq = freq_ref[:, core].reshape(rows, depth)
        ratio = omega_ref[:, core].reshape(rows, depth) / freq
        for energy in range(out_ref.shape[1]):
            gap = shift_ref[energy, 0:1, :] - freq
            out_ref[core, energy] = ratio * gap / (gap * gap + 0.09)


def half_terms(z_lo, core, kern_ref, blocks_ref, left_ref):
    chips = left_ref.shape[0]
    for i, at_z in enumerate((z_lo, 1 - z_lo)):
        left_ref[:FAR_FIRST, at_z] = blocks_ref[i, chips - FAR_FIRST :]
        left_ref[FAR_FIRST:, at_z] = blocks_ref[i, : chips - FAR_FIRST]
    left = left_ref[...].reshape(-1, left_ref.shape[-1]).T
    for energy in range(kern_ref.shape[1]):
        yield dot(left, kern_ref[core, energy])


def mine_body(place_ref, kern_ref, mine_ref, out_ref, left_ref):
    z_lo, core = place_ref[0], place_ref[1]
    for energy, term in enumerate(half_terms(z_lo, core, kern_ref, mine_ref, left_ref)):
        out_ref[energy] = term


def rest_body(place_ref, kern_ref, other_ref, part_ref, out_ref, left_ref):
    z_lo, core = place_ref[0], place_ref[1]
    for energy, term in enumerate(half_terms(z_lo, 1 - core, kern_ref, other_ref, left_ref)):
        out_ref[energy] = part_ref[energy] + term


def last_body(part_ref, right_ref, out_ref):
    lines, lanes = out_ref.shape[2:]
    for energy in range(part_ref.shape[0]):
        out_ref[:, energy] = dot(part_ref[energy], right_ref[...]).reshape(-1, lines, lanes)


def local_kernel(body, out_shape, flops, arrays, scratch=()):
    spaces = [pltpu.SMEM if a.dtype == jnp.int32 else pltpu.VMEM for a in arrays]
    return pl.pallas_call(
        body,
        out_shape=jax.ShapeDtypeStruct(out_shape, jnp.float32),
        in_specs=[pl.BlockSpec(memory_space=space) for space in spaces],
        out_specs=pl.BlockSpec(memory_space=pltpu.VMEM),
        scratch_shapes=scratch,
        compiler_params=pltpu.CompilerParams(vmem_limit_bytes=16 << 20),
        cost_estimate=pl.CostEstimate(
            flops=flops,
            bytes_accessed=4 * (sum(a.size for a in arrays) + math.prod(out_shape)),
            transcendentals=0,
        ),
    )(*arrays)


def exchange(pieces, axes, first):
    size = pieces.shape[0]
    order = [(first + i) % size for i in range(size)]
    return lax.all_to_all(pieces, axes, 0, 0, axis_index_groups=[order])


def gather(block, axes, first):
    size = lax.axis_size(axes)
    return exchange(jnp.broadcast_to(block, (size, *block.shape)), axes, first)


def sum_everywhere(tiles):
    size = lax.axis_size(NEAR)
    lanes = tiles.shape[-1]
    pieces = exchange(tiles.reshape(size, -1, 2, lanes), NEAR, NEAR_FIRST)
    piece = jnp.sum(gather(jnp.sum(pieces, axis=0), "z_far", FAR_FIRST), axis=0)
    return gather(piece, NEAR, NEAR_FIRST).reshape(tiles.shape)


def with_partner(blocks, axis):
    return jnp.stack([blocks, lax.ppermute(blocks, axis, ((0, 1), (1, 0)))])


def shards(omega_sq, pole_freq, mtx_left, mtx_right, band_ids, band_energy, eval_energy):
    table = band_energy.shape[0]
    energies = eval_energy.shape[0]
    states = mtx_left.shape[2]
    depth = pole_freq.shape[1]
    place = jnp.stack([lax.axis_index("z_lo"), lax.axis_index("core")])
    pairs = (-1, 2, mtx_left.shape[1], depth)
    omega, freq = omega_sq.reshape(pairs), pole_freq.reshape(pairs)
    hits = (band_ids[:, None] == jnp.arange(table, dtype=jnp.int32)[None, :]).astype(jnp.float32)
    levels = jnp.sum(hits * band_energy[None, :], axis=1)
    shifts = eval_energy[None, :] - levels[:, None]
    shift_rows = jnp.broadcast_to(shifts[0][:, None, None], (energies, 8, depth))
    left_far = gather(mtx_left[0], "z_far", FAR_FIRST)
    mine = with_partner(left_far, "z_lo")
    other = lax.ppermute(mine, "core", ((0, 1), (1, 0)))
    right_blocks = gather(mtx_right[0], ROW, ROW_FIRST)
    right_cols = jnp.roll(right_blocks, ROW_FIRST, axis=0).reshape(-1, states)
    shape = (2, energies, freq.size // depth // 2, depth)
    kern = local_kernel(kern_body, shape, 8 * energies * freq.size, (shift_rows, omega, freq))
    left_rows = pltpu.VMEM((mine.shape[1], mine.shape[0], *mine.shape[2:]), jnp.float32)
    flops = kern.size * states
    shape = (energies, states, depth)
    part = local_kernel(mine_body, shape, flops, (place, kern, mine), (left_rows,))
    part = local_kernel(rest_body, shape, flops, (place, kern, other, part), (left_rows,))
    shape = (states // 8, energies, 8, states)
    tiles = local_kernel(last_body, shape, 2 * part.size * states, (part, right_cols))
    return sum_everywhere(tiles).transpose(0, 2, 1, 3).reshape(states, energies * states)


def solution(mesh):
    split = Mesh(mesh.devices.reshape(4, 4, 16, 2, 2), (*ROW, *COL))
    return jax.shard_map(
        shards,
        mesh=split,
        in_specs=(
            P(ROW, COL),
            P(ROW, COL),
            P(None, (*ROW, *COL), None),
            P(None, (*COL, *ROW), None),
            P(),
            P(),
            P(),
        ),
        out_specs=P(),
        check_vma=False,
    )
```

```python
import math

import jax
import jax.numpy as jnp
from jax import lax
from jax.experimental import pallas as pl
from jax.experimental.pallas import tpu as pltpu
from jax.sharding import Mesh, PartitionSpec as P


ROW = ("x", "y")
COL = ("z_far", "z_lo", "core")
NEAR = (*ROW, "z_lo", "core")
ROW_FIRST = 2 * 4 + 2
NEAR_FIRST = (ROW_FIRST * 2 + 1) * 2
FAR_FIRST = 9


def dot(left, right):
    return jnp.dot(
        left,
        right,
        precision=lax.Precision.HIGHEST,
        preferred_element_type=jnp.float32,
    )


def kern_body(shift_ref, omega_ref, freq_ref, out_ref):
    rows = out_ref.shape[1]
    depth = freq_ref.shape[-1]
    for core in range(out_ref.shape[0]):
        freq = freq_ref[:, core].reshape(rows, depth)
        ratio = omega_ref[:, core].reshape(rows, depth) / freq
        for energy in range(shift_ref.shape[0]):
            gap = shift_ref[energy, 0:1, :] - freq
            out_ref[core, :, energy * depth : (energy + 1) * depth] = ratio * gap / (gap * gap + 0.09)


def half_term(z_lo, core, kern_ref, blocks_ref, left_ref):
    chips = left_ref.shape[0]
    for i, at_z in enumerate((z_lo, 1 - z_lo)):
        left_ref[:FAR_FIRST, at_z] = blocks_ref[i, chips - FAR_FIRST :]
        left_ref[FAR_FIRST:, at_z] = blocks_ref[i, : chips - FAR_FIRST]
    return dot(left_ref[...].reshape(-1, left_ref.shape[-1]).T, kern_ref[core])


def mine_body(place_ref, kern_ref, mine_ref, out_ref, left_ref):
    out_ref[...] = half_term(place_ref[0], place_ref[1], kern_ref, mine_ref, left_ref)


def rest_body(place_ref, kern_ref, other_ref, part_ref, out_ref, left_ref):
    term = half_term(place_ref[0], 1 - place_ref[1], kern_ref, other_ref, left_ref)
    out_ref[...] = part_ref[...] + term


def last_body(part_ref, right_ref, out_ref):
    lines, lanes = out_ref.shape[2:]
    depth = right_ref.shape[0]
    for energy in range(out_ref.shape[1]):
        part = part_ref[:, energy * depth : (energy + 1) * depth]
        out_ref[:, energy] = dot(part, right_ref[...]).reshape(-1, lines, lanes)


def local_kernel(body, out_shape, flops, arrays, scratch=()):
    spaces = [pltpu.SMEM if a.dtype == jnp.int32 else pltpu.VMEM for a in arrays]
    return pl.pallas_call(
        body,
        out_shape=jax.ShapeDtypeStruct(out_shape, jnp.float32),
        in_specs=[pl.BlockSpec(memory_space=space) for space in spaces],
        out_specs=pl.BlockSpec(memory_space=pltpu.VMEM),
        scratch_shapes=scratch,
        compiler_params=pltpu.CompilerParams(vmem_limit_bytes=16 << 20),
        cost_estimate=pl.CostEstimate(
            flops=flops,
            bytes_accessed=4 * (sum(a.size for a in arrays) + math.prod(out_shape)),
            transcendentals=0,
        ),
    )(*arrays)


def exchange(pieces, axes, first):
    size = pieces.shape[0]
    order = [(first + i) % size for i in range(size)]
    return lax.all_to_all(pieces, axes, 0, 0, axis_index_groups=[order])


def gather(block, axes, first):
    size = lax.axis_size(axes)
    return exchange(jnp.broadcast_to(block, (size, *block.shape)), axes, first)


def sum_everywhere(tiles):
    size = lax.axis_size(NEAR)
    lanes = tiles.shape[-1]
    pieces = exchange(tiles.reshape(size, -1, 2, lanes), NEAR, NEAR_FIRST)
    piece = jnp.sum(gather(jnp.sum(pieces, axis=0), "z_far", FAR_FIRST), axis=0)
    return gather(piece, NEAR, NEAR_FIRST).reshape(tiles.shape)


def with_partner(blocks, axis):
    return jnp.stack([blocks, lax.ppermute(blocks, axis, ((0, 1), (1, 0)))])


def shards(omega_sq, pole_freq, mtx_left, mtx_right, band_ids, band_energy, eval_energy):
    table = band_energy.shape[0]
    energies = eval_energy.shape[0]
    states = mtx_left.shape[2]
    depth = pole_freq.shape[1]
    place = jnp.stack([lax.axis_index("z_lo"), lax.axis_index("core")])
    pairs = (-1, 2, mtx_left.shape[1], depth)
    omega, freq = omega_sq.reshape(pairs), pole_freq.reshape(pairs)
    hits = (band_ids[:, None] == jnp.arange(table, dtype=jnp.int32)[None, :]).astype(jnp.float32)
    levels = jnp.sum(hits * band_energy[None, :], axis=1)
    shifts = eval_energy[None, :] - levels[:, None]
    shift_rows = jnp.broadcast_to(shifts[0][:, None, None], (energies, 8, depth))
    left_far = gather(mtx_left[0], "z_far", FAR_FIRST)
    mine = with_partner(left_far, "z_lo")
    other = lax.ppermute(mine, "core", ((0, 1), (1, 0)))
    right_blocks = gather(mtx_right[0], ROW, ROW_FIRST)
    right_cols = jnp.roll(right_blocks, ROW_FIRST, axis=0).reshape(-1, states)
    shape = (2, freq.size // depth // 2, energies * depth)
    kern = local_kernel(kern_body, shape, 8 * energies * freq.size, (shift_rows, omega, freq))
    left_rows = pltpu.VMEM((mine.shape[1], mine.shape[0], *mine.shape[2:]), jnp.float32)
    flops = kern.size * states
    shape = (states, energies * depth)
    part = local_kernel(mine_body, shape, flops, (place, kern, mine), (left_rows,))
    part = local_kernel(rest_body, shape, flops, (place, kern, other, part), (left_rows,))
    shape = (states // 8, energies, 8, states)
    tiles = local_kernel(last_body, shape, 2 * part.size * states, (part, right_cols))
    return sum_everywhere(tiles).transpose(0, 2, 1, 3).reshape(states, energies * states)


def solution(mesh):
    split = Mesh(mesh.devices.reshape(4, 4, 16, 2, 2), (*ROW, *COL))
    return jax.shard_map(
        shards,
        mesh=split,
        in_specs=(
            P(ROW, COL),
            P(ROW, COL),
            P(None, (*ROW, *COL), None),
            P(None, (*COL, *ROW), None),
            P(),
            P(),
            P(),
        ),
        out_specs=P(),
        check_vma=False,
    )
```
